32 devices in a mesh: mem: 16 (over z, y, core), lat: 2 (over x).
Axes of the slice: x: 2, y: 2, z: 4, core: 2. Of those that a mesh axis runs over, the one named last changes fastest.
Arguments:
- controls: bfloat16 [64, 64, 256, 256], P('mem', None, 'lat'), may hold values from -6 to 6
- spread: bfloat16 [64, 64, 256, 256], P('mem', None, 'lat'), may hold values from -1.5 to 1.5
- classes: int32 [256, 256], P('lat'), may hold values from 0 to 7
- prec_table: float32 [8, 64], replicated, may hold values from 0.25 to 4
- vert_loc: bfloat16 [64, 64], replicated, may hold values from 0 to 1
- lon_loc: bfloat16 [256, 256], replicated, may hold values from 0 to 1
- lat_loc: bfloat16 [256, 256], replicated, may hold values from 0 to 1
Outputs:
- localized: bfloat16 [64, 64, 256, 256], P('mem', None, 'lat')
The draws below stay inside these ranges and needn't reach their ends.
All inputs are finite; a program needn't handle non-finite values.
Results may differ from the reference program's by a relative error of at most 0.0064.
Values may be sent and summed in bfloat16 or wider, within the bound.
A program may use at most 128 MiB of HBM per device.

```python
import math
import jax
import jax.numpy as jnp
from jax import lax

LEV = 64
LAT = 256
LON = 256
NCLASS = 8
MEMBERS = 64


def draw_range():
    return (0.5, 1.5, 0.6)


def banded(key, size, reach):
    lower, upper, centre = draw_range()
    positions = jnp.arange(size)
    distance = jnp.abs(positions[:, None] - positions[None, :]).astype(jnp.float32)
    noise = jax.random.uniform(key, (size, size), jnp.float32, lower, upper)
    offdiag = jnp.exp(-distance / float(reach)) * noise / (4.0 * float(reach))
    return jnp.where(distance == 0.0, centre + 0.05 * noise, offdiag)


def draw_vert_loc(key, part):
    return banded(jax.random.fold_in(key, 11), LEV, LEV // 4).astype(jnp.bfloat16)


def draw_lon_loc(key, part):
    return banded(jax.random.fold_in(key, 23), LON, LON // 4).astype(jnp.bfloat16)


def draw_lat_loc(key, part):
    return banded(jax.random.fold_in(key, 37), LAT, LAT // 4).astype(jnp.bfloat16)


def plant(array, own_key, smallest, top_value):
    longest = array.shape.index(max(array.shape))
    spots = []
    for shift in (0, 1):
        where = [jax.random.randint(jax.random.fold_in(own_key, axis), (), 0, length) for axis, length in enumerate(array.shape)]
        where[longest] = (where[longest] + shift) % array.shape[longest]
        spots.append(tuple(where))
    return array.at[spots[0]].set(smallest).at[spots[1]].set(top_value)


def steps_of(key, dims, pieces, low, largest):
    def one(axis_at, parts):
        heights = jax.random.uniform(jax.random.fold_in(jax.random.fold_in(key, 6), axis_at), (parts,), jnp.float32, low / len(pieces), largest / len(pieces))
        return jnp.repeat(jnp.exp(heights), dims[axis_at] // parts).reshape((-1,) + (1,) * (len(dims) - axis_at - 1))

    factor_of = one(*pieces[0])
    for cut in pieces[1:]:
        factor_of = factor_of * one(*cut)
    return factor_of


def normal_values(key, shape, width, most, shards=(), kind=jnp.bfloat16):
    values = width * jax.random.normal(key, shape, jnp.float32)
    if shards:
        values = values * steps_of(key, shape, shards, -0.22, 0.18)
    return jnp.clip(values, -most, most).astype(kind)


def setup_inputs(seed: int = 0) -> dict:
    key_of = jax.random.split(jax.random.key(seed), 8)
    controls = normal_values(key_of[0], (MEMBERS, LEV, LAT, LON), 1.0, 6.0, ((0, 16), (2, 2)))
    spread = normal_values(key_of[1], (MEMBERS, LEV, LAT, LON), 0.25, 1.5, ((0, 16), (2, 2)))
    classes = plant(jax.random.randint(key_of[2], (LAT, LON), 0, NCLASS), jax.random.fold_in(key_of[2], 1), 0, NCLASS - 1).astype(jnp.int32)
    prec_table = jnp.clip(jnp.exp(jax.random.uniform(key_of[3], (NCLASS, LEV), jnp.float32, math.log(0.25), math.log(4.0))), 0.25, 4.0)
    vert_loc = draw_vert_loc(jax.random.fold_in(key_of[7], 71), 0)
    lon_loc = draw_lon_loc(jax.random.fold_in(key_of[7], 71), 0)
    lat_loc = draw_lat_loc(jax.random.fold_in(key_of[7], 71), 0)
    return dict(controls=controls, spread=spread, classes=classes, prec_table=prec_table, vert_loc=vert_loc, lon_loc=lon_loc, lat_loc=lat_loc)


def lookup(table, classes):
    numbers = jnp.arange(table.shape[0], dtype=jnp.int32)
    onehot = (classes[None, :, :] == numbers[:, None, None]).astype(jnp.float32)
    return jnp.einsum("kl,kab->lab", table, onehot, precision=lax.Precision.HIGHEST)


def reference(controls, spread, classes, prec_table, vert_loc, lon_loc, lat_loc):
    def accumulate(total, pair):
        member_spread, member_ctrl = pair
        return total + member_spread.astype(jnp.float32) * member_ctrl.astype(jnp.float32), None

    start = jnp.zeros(controls.shape[1:], jnp.float32)
    increment, _ = lax.scan(accumulate, start, (spread, controls))
    weighted = increment * lookup(prec_table, classes)
    vert_f = vert_loc.astype(jnp.float32)
    lon_f = lon_loc.astype(jnp.float32)
    lat_f = lat_loc.astype(jnp.float32)

    def member(member_spread):
        adjoint = (member_spread.astype(jnp.float32) * weighted).astype(jnp.bfloat16)
        along_lon = jnp.einsum("lac,bc->lab", adjoint.astype(jnp.float32), lon_f, precision=lax.Precision.HIGHEST).astype(jnp.bfloat16)
        along_lev = jnp.einsum("lj,jab->lab", vert_f, along_lon.astype(jnp.float32), precision=lax.Precision.HIGHEST).astype(jnp.bfloat16)
        return jnp.einsum("ac,lcb->lba", lat_f, along_lev.astype(jnp.float32), precision=lax.Precision.HIGHEST).astype(jnp.bfloat16)

    return lax.map(member, spread)
```

```python
import functools

import jax
import jax.numpy as jnp
from jax import lax
from jax.experimental import pallas as pl
from jax.experimental.pallas import tpu as pltpu
from jax.sharding import PartitionSpec as P

CHUNKS = 4
MIN_ROWS = 16
LANES = 128


def lookup(table, classes):
    numbers = jnp.arange(table.shape[0], dtype=jnp.int32)
    onehot = (classes[None, :, :] == numbers[:, None, None]).astype(jnp.float32)
    return jnp.einsum("kl,kab->lab", table, onehot, precision=lax.Precision.HIGHEST)


def last_kernel(count, *refs):
    pieces, weights_ref, out_ref = refs[:count], refs[count], refs[count + 1]
    weights = weights_ref[...]
    for level in range(out_ref.shape[1]):
        rows = jnp.concatenate([piece[0, level] for piece in pieces], axis=0)
        out_ref[0, level] = jnp.dot(
            rows.T, weights, preferred_element_type=jnp.float32
        ).astype(out_ref.dtype)


def along_lat(pieces, weights, levels_per_step=8):
    members, levels, _, width = pieces[0].shape
    step = min(levels_per_step, levels)
    total = weights.shape[1]
    in_specs = [
        pl.BlockSpec((1, step, piece.shape[2], width), lambda m, l: (m, l, 0, 0))
        for piece in pieces
    ] + [pl.BlockSpec(weights.shape, lambda m, l: (0, 0))]
    return pl.pallas_call(
        functools.partial(last_kernel, len(pieces)),
        grid=(members, levels // step),
        out_shape=jax.ShapeDtypeStruct((members, levels, width, total), jnp.bfloat16),
        in_specs=in_specs,
        out_specs=pl.BlockSpec((1, step, width, total), lambda m, l: (m, l, 0, 0)),
        compiler_params=pltpu.CompilerParams(
            dimension_semantics=("arbitrary", "arbitrary")
        ),
    )(*pieces, weights)


def sum_kernel(spread_ref, controls_ref, out_ref):
    total = spread_ref[0].astype(jnp.float32) * controls_ref[0].astype(jnp.float32)
    for member in range(1, spread_ref.shape[0]):
        total += spread_ref[member].astype(jnp.float32) * controls_ref[member].astype(jnp.float32)
    out_ref[...] = total


def member_sum(spread, controls, chunk, rows, levels_per_step=16):
    members, levels, _, cols = spread.shape
    step = min(levels_per_step, levels)
    block = pl.BlockSpec((members, step, rows, cols), lambda l: (0, l, chunk, 0))
    size = members * levels * rows * cols
    return pl.pallas_call(
        sum_kernel,
        grid=(levels // step,),
        out_shape=jax.ShapeDtypeStruct((levels, rows, cols), jnp.float32),
        in_specs=[block, block],
        out_specs=pl.BlockSpec((step, rows, cols), lambda l: (l, 0, 0)),
        cost_estimate=pl.CostEstimate(flops=2 * size, bytes_accessed=5 * size, transcendentals=0),
        compiler_params=pltpu.CompilerParams(dimension_semantics=("arbitrary",)),
    )(spread, controls)


def middle_kernel(width, spread_ref, weighted_ref, lon_ref, vert_ref, *refs):
    total = lon_ref.shape[1]
    pieces, groups = total // width, total // LANES
    out_refs = refs[:pieces]
    before, after = refs[pieces : pieces + groups], refs[pieces + groups :]
    _, levels, rows, cols = spread_ref.shape
    adjoint = (
        spread_ref[0].astype(jnp.float32) * weighted_ref[...].astype(jnp.float32)
    ).astype(jnp.bfloat16)
    along_lon = (
        jnp.dot(
            adjoint.reshape(levels * rows, cols), lon_ref[...], preferred_element_type=jnp.float32
        )
        .astype(jnp.bfloat16)
        .astype(jnp.float32)
    )
    for g in range(groups):
        before[g][...] = along_lon[:, g * LANES : (g + 1) * LANES]
    vert = vert_ref[...]
    for row in range(rows):
        strided = pl.ds(row, levels, stride=rows)
        column = jnp.concatenate([half[strided, :] for half in before], axis=1)
        along_lev = jnp.dot(
            vert, column.astype(jnp.bfloat16), preferred_element_type=jnp.float32
        )
        for g in range(groups):
            after[g][strided, :] = along_lev[:, g * LANES : (g + 1) * LANES]
    joined = jnp.concatenate([half[...] for half in after], axis=1).astype(jnp.bfloat16)
    for s, out_ref in enumerate(out_refs):
        out_ref[0] = joined[:, s * width : (s + 1) * width].reshape(levels, rows, width)


def lon_and_lev(spread, weighted, lon_columns, vert_loc, chunk, rows, width):
    members, levels, _, cols = spread.shape
    total = lon_columns.shape[1]
    pieces = total // width
    size = members * levels * rows * cols
    return pl.pallas_call(
        functools.partial(middle_kernel, width),
        grid=(members,),
        out_shape=[jax.ShapeDtypeStruct((members, levels, rows, width), jnp.bfloat16)] * pieces,
        in_specs=[
            pl.BlockSpec((1, levels, rows, cols), lambda m: (m, 0, chunk, 0)),
            pl.BlockSpec(weighted.shape, lambda m: (0, 0, 0)),
            pl.BlockSpec(lon_columns.shape, lambda m: (0, 0)),
            pl.BlockSpec(vert_loc.shape, lambda m: (0, 0)),
        ],
        out_specs=[pl.BlockSpec((1, levels, rows, width), lambda m: (m, 0, 0, 0))] * pieces,
        scratch_shapes=[pltpu.VMEM((levels * rows, LANES), jnp.float32)] * (2 * total // LANES),
        cost_estimate=pl.CostEstimate(
            flops=2 * size * (cols + levels), bytes_accessed=4 * size, transcendentals=0
        ),
        compiler_params=pltpu.CompilerParams(dimension_semantics=("arbitrary",)),
    )(spread, weighted, lon_columns, vert_loc)


def local(mem_count, lat_count, controls, spread, classes, prec_table, vert_loc, lon_loc, lat_loc):
    levels, rows = controls.shape[1:3]
    width = lon_loc.shape[0] // lat_count
    here, member_at = lax.axis_index("lat"), lax.axis_index("mem")
    chunk_rows = max(min(MIN_ROWS, rows), rows // CHUNKS)
    chunks = rows // chunk_rows
    lon_all = jnp.concatenate(
        [
            lax.dynamic_slice_in_dim(lon_loc, lax.rem(here + s, lat_count) * width, width, 0)
            for s in range(lat_count)
        ],
        axis=0,
    ).T
    strides, stride = [], 1
    while stride < mem_count:
        strides.append(stride)
        stride *= 2
    bits = [lax.rem(lax.div(member_at, stride), 2) for stride in strides]

    def swap(value, stride):
        return lax.ppermute(value, "mem", [(i, i ^ stride) for i in range(mem_count)])

    first, size = 0, levels
    for bit in bits:
        size //= 2
        first = first + bit * size
    table_rows = lax.dynamic_slice_in_dim(prec_table, first, size, 1)

    def weighted_of(k):
        total = member_sum(spread, controls, k, chunk_rows)
        for bit, stride in zip(bits, strides):
            half = total.shape[0] // 2
            keep = lax.dynamic_slice_in_dim(total, bit * half, half, 0)
            away = lax.dynamic_slice_in_dim(total, (1 - bit) * half, half, 0)
            total = keep + swap(away.astype(jnp.bfloat16), stride).astype(jnp.float32)
        part = classes[k * chunk_rows : (k + 1) * chunk_rows]
        value = (total * lookup(table_rows, part)).astype(jnp.bfloat16)
        for bit, stride in reversed(list(zip(bits, strides))):
            other = swap(value, stride)
            value = jnp.where(
                bit == 0,
                jnp.concatenate([value, other], axis=0),
                jnp.concatenate([other, value], axis=0),
            )
        return value

    got = [[] for _ in range(lat_count)]
    for k in range(chunks):
        blocks = lon_and_lev(spread, weighted_of(k), lon_all, vert_loc, k, chunk_rows, width)
        for s in range(lat_count):
            block = blocks[s]
            if s:
                block = lax.ppermute(
                    block, "lat", [(i, (i + s) % lat_count) for i in range(lat_count)]
                )
            got[s].append(block)
    lat_columns = jnp.concatenate(
        [
            lax.dynamic_slice_in_dim(
                lat_loc, lax.rem(here + lat_count - s, lat_count) * rows, rows, 1
            )
            for s in range(lat_count)
        ],
        axis=1,
    )
    return along_lat([piece for group in got for piece in group], lat_columns.T)


def solution(mesh):
    return jax.shard_map(
        functools.partial(local, mesh.shape["mem"], mesh.shape["lat"]),
        mesh=mesh,
        in_specs=(
            P("mem", None, "lat", None),
            P("mem", None, "lat", None),
            P("lat", None),
            P(),
            P(),
            P(),
            P(),
        ),
        out_specs=P("mem", None, "lat", None),
        check_vma=False,
    )
```
